32 devices in a mesh: seq: 8 (over z, y), head: 4 (over x, core).
Axes of the slice: x: 2, y: 2, z: 4, core: 2. Of those that a mesh axis runs over, the one named last changes fastest.
Arguments:
- queries: bfloat16 [1024, 3584], P('seq', 'head'), may hold values from -256 to 256
- key_codes: bfloat16 [1024, 512], P('seq', 'head'), may hold values from -4 to 4
- value_codes: bfloat16 [1024, 512], P('seq', 'head'), may hold values from -4 to 4
- kv_scales: float32 [2, 8, 4], P(None, 'seq', 'head'), may hold values from 0.5 to 2
- out_weight: bfloat16 [3584, 3584], P('head'), may hold values from -0.09375 to 0.09375
- turn_ids: int32 [1024], replicated, may hold values from 0 to 7, never falling along the last dimension, each value on 1 to 256 neighbouring positions
- block_mask: int32 [8, 8], P('seq'), may hold values 0 or 1
- doc_lengths: int32 [4], replicated, may hold values from 1 to 512, 1024 in all
Outputs:
- projected: bfloat16 [1024, 3584], P('seq', 'head')
The draws below stay inside these ranges and needn't reach their ends.
All inputs are finite; a program needn't handle non-finite values. No bound on the sum of `block_mask` on one device may be relied on, other than what follows from the above.
Results may differ from the reference program's by a relative error of at most 0.012.
Values may be sent and summed in bfloat16 or wider, within the bound.
No kernel may reach another device: no remote copies, remote signals or barrier semaphores. Data moves between devices by JAX's collectives and lax.ppermute only.
A program may use at most 128 MiB of HBM per device.

```python
import math
import jax
import jax.numpy as jnp
import numpy as np
from jax import lax

D = 3584
QHEADS = 28
KVH = 4
HEAD_DIM = 128
BLOCK = 128
TURN_MOST = 256
NDOC = 4
TOKENS = 1024
NBLOCKS = 8
TURNS = 8


def shared_keys(key):
    code_key = jax.random.fold_in(key, 11)
    scale_key = jax.random.fold_in(key, 12)
    codes = jnp.clip(jax.random.normal(code_key, (TOKENS, KVH * HEAD_DIM), jnp.float32), -4.0, 4.0)
    scales = jnp.exp(jax.random.uniform(scale_key, (2, TOKENS // BLOCK, KVH), jnp.float32, math.log(0.5), math.log(2.0)))
    return (codes, scales)


def draw_key_codes(key, part):
    return shared_keys(key)[0].astype(jnp.bfloat16)


def draw_kv_scales(key, part):
    return shared_keys(key)[1]


def draw_queries(key, part):
    base = jnp.clip(jax.random.normal(jax.random.fold_in(key, 21), (TOKENS, QHEADS * HEAD_DIM), jnp.float32), -4.0, 4.0)
    return base.astype(jnp.bfloat16)


def place_ends(entries, stream_key, smallest, largest):
    spot = [jax.random.randint(jax.random.fold_in(stream_key, axis), (), 0, length) for axis, length in enumerate(entries.shape)]
    main_axis = entries.shape.index(max(entries.shape))
    neighbour = spot[:main_axis] + [(spot[main_axis] + 1) % entries.shape[main_axis]] + spot[main_axis + 1:]
    return entries.at[tuple(spot)].set(smallest).at[tuple(neighbour)].set(largest)


def block_levels(stream_key, extent, shards, smallest, high):
    level = 1.0
    for dim, parts in shards:
        draws = jax.random.uniform(jax.random.fold_in(jax.random.fold_in(stream_key, 6), dim), (parts,), jnp.float32, smallest / len(shards), high / len(shards))
        level = level * jnp.repeat(jnp.exp(draws), extent[dim] // parts).reshape((-1,) + (1,) * (len(extent) - 1 - dim))
    return level


def profile(number_of, total, limit, slope):
    weights = [(1 << 20) // math.isqrt(rank ** slope) + 1 for rank in range(2, number_of + 1)]
    spare, counts = total - limit - (number_of - 1), [1] * (number_of - 1)
    while spare > 0:
        free = [i for i in range(number_of - 1) if counts[i] < limit]
        whole, remaining = sum([weights[i] for i in free]), spare
        for i in free:
            addition = min(limit - counts[i], max(1, remaining * weights[i] // whole), spare)
            counts[i] = counts[i] + addition
            spare = spare - addition
    return np.array([limit] + counts)


def ragged_sizes(key, amount, total, most, lean):
    if amount == 2:
        one = jax.random.randint(key, (), max(1, total - most), min(most, total - 1) + 1)
        return jnp.stack([one, total - one])
    tallies = jnp.asarray(profile(amount, total, most, lean), jnp.int32)
    couples = (amount - 1) // 2
    giver, sink = tallies[1:1 + 2 * couples:2], tallies[2:2 + 2 * couples:2]
    slack = jnp.minimum(giver - 1, most - sink)
    moved = jax.random.randint(jax.random.fold_in(key, 1), (couples,), 0, 1 << 20) % (slack + 1)
    tallies = tallies.at[1:1 + 2 * couples:2].set(giver - moved).at[2:2 + 2 * couples:2].set(sink + moved)
    return tallies[jax.random.permutation(jax.random.fold_in(key, 2), amount)]


def bell_draw(key, extent, scale, limit, shards=(), kind=jnp.bfloat16):
    values = scale * jax.random.normal(key, extent, jnp.float32)
    if shards:
        values = values * block_levels(key, extent, shards, -0.22, 0.18)
    return jnp.clip(values, -limit, limit).astype(kind)


def setup_inputs(seed: int = 0) -> dict:
    arg_keys = jax.random.split(jax.random.key(seed), 9)
    queries = draw_queries(jax.random.fold_in(arg_keys[8], 71), 0)
    key_codes = draw_key_codes(jax.random.fold_in(arg_keys[8], 71), 0)
    value_codes = bell_draw(arg_keys[2], (TOKENS, KVH * HEAD_DIM), 1.0, 4.0, ((0, 8), (1, 4)))
    kv_scales = draw_kv_scales(jax.random.fold_in(arg_keys[8], 71), 0)
    out_weight = bell_draw(arg_keys[4], (QHEADS * HEAD_DIM, D), (QHEADS * HEAD_DIM) ** -0.5, 0.09375, ((0, 4),))
    turn_ids = jnp.searchsorted(jnp.cumsum(ragged_sizes(arg_keys[5], TURNS, TOKENS, TURN_MOST, 1)), jnp.arange(TOKENS), side="right").astype(jnp.int32)
    block_mask = place_ends((jax.random.randint(arg_keys[6], (NBLOCKS, NBLOCKS), 0, 100) < 3).astype(jnp.int32), jax.random.fold_in(arg_keys[6], 1), 0, 1)
    doc_lengths = ragged_sizes(arg_keys[7], NDOC, TOKENS, TOKENS // 2, 1).astype(jnp.int32)
    return dict(queries=queries, key_codes=key_codes, value_codes=value_codes, kv_scales=kv_scales, out_weight=out_weight, turn_ids=turn_ids, block_mask=block_mask, doc_lengths=doc_lengths)


masked_score = -1e+30

def document_of(places, doc_lengths):
    ends = jnp.cumsum(doc_lengths)
    return lax.optimization_barrier(jnp.sum((places[:, None] >= ends[None, :]).astype(jnp.int32), axis=1))

def reference(queries, key_codes, value_codes, kv_scales, out_weight, turn_ids, block_mask, doc_lengths):
    groups = QHEADS // KVH
    key_scale = jnp.repeat(kv_scales[0], BLOCK, axis=0)
    value_scale = jnp.repeat(kv_scales[1], BLOCK, axis=0)
    keys = (key_codes.astype(jnp.float32).reshape(TOKENS, KVH, HEAD_DIM) * key_scale[:, :, None]).astype(jnp.bfloat16)
    values = (value_codes.astype(jnp.float32).reshape(TOKENS, KVH, HEAD_DIM) * value_scale[:, :, None]).astype(jnp.bfloat16)
    keys = lax.optimization_barrier(keys).astype(jnp.float32)
    values = lax.optimization_barrier(values).astype(jnp.float32)
    places = jnp.arange(TOKENS, dtype=jnp.int32)
    docs = document_of(places, doc_lengths)
    scaling = 1.0 / math.sqrt(HEAD_DIM)
    query_blocks = queries.reshape(NBLOCKS, BLOCK, KVH, groups, HEAD_DIM)

    def one_block(inputs):
        block_rows, index = inputs
        query_places = index * BLOCK + jnp.arange(BLOCK, dtype=jnp.int32)
        query_docs = lax.dynamic_slice_in_dim(docs, index * BLOCK, BLOCK)
        query_turns = lax.dynamic_slice_in_dim(turn_ids, index * BLOCK, BLOCK)
        mask_row = lax.dynamic_slice_in_dim(block_mask, index, 1, 0)[0]
        kept = jnp.repeat(mask_row, BLOCK) > 0
        same_block = places // BLOCK == index
        allowed = (places[None, :] <= query_places[:, None]) & (query_docs[:, None] == docs[None, :]) & ((query_turns[:, None] == turn_ids[None, :]) | kept[None, :] | same_block[None, :])
        scores = jnp.einsum('qhgd,khd->hgqk', block_rows.astype(jnp.float32), keys) * scaling
        scores = jnp.where(allowed[None, None], scores, masked_score)
        best = lax.optimization_barrier(jnp.max(scores, axis=3, keepdims=True))
        weights = jnp.where(allowed[None, None], jnp.exp(scores - best), 0.0)
        totals = lax.optimization_barrier(jnp.sum(weights, axis=3))
        rounded = lax.optimization_barrier(weights.astype(jnp.bfloat16)).astype(jnp.float32)
        summed = jnp.einsum('hgqk,khd->qhgd', rounded, values)
        result = summed / jnp.transpose(totals, (2, 0, 1))[:, :, :, None]
        return result.astype(jnp.bfloat16).reshape(BLOCK, QHEADS * HEAD_DIM)
    attended = lax.map(one_block, (query_blocks, jnp.arange(NBLOCKS, dtype=jnp.int32)))
    attended = attended.reshape(TOKENS, QHEADS * HEAD_DIM)
    return jnp.dot(attended, out_weight, preferred_element_type=jnp.float32).astype(jnp.bfloat16)
```

```python
import functools
import math

import jax
import jax.numpy as jnp
from jax import lax
from jax.experimental import pallas as pl
from jax.experimental.pallas import tpu as pltpu
from jax.sharding import PartitionSpec as P

masked_score = -1e30


def whole(space=pltpu.VMEM):
    return pl.BlockSpec(memory_space=space)


def cost(flops, moved):
    return pl.CostEstimate(flops=flops, bytes_accessed=moved, transcendentals=0)


def dequantize_kernel(scales_ref, keys_ref, values_ref, pair_ref):
    rows = keys_ref.shape[0]
    pair_ref[:rows] = (keys_ref[...].astype(jnp.float32) * scales_ref[0]).astype(jnp.bfloat16)
    pair_ref[rows:] = (values_ref[...].astype(jnp.float32) * scales_ref[1]).astype(jnp.bfloat16)


def slots_of(mine, count):
    other = mine ^ 1
    held = [mine, other]
    for step in range(1, count // 4 + 1):
        held += [lax.rem(mine - 2 * step + count, count), lax.rem(other - 2 * step + count, count)]
    return held


def mask_kernel(count, lengths_ref, blocks_ref, turns_ref, bias_ref):
    rows = bias_ref.shape[1]
    mine = lax.axis_index("seq")
    row = lax.broadcasted_iota(jnp.int32, (rows, rows), 0)
    column = lax.broadcasted_iota(jnp.int32, (rows, rows), 1)
    place = mine * rows + row
    start = jnp.zeros((rows, rows), jnp.int32)
    end = jnp.int32(0)
    for doc in range(lengths_ref.shape[0]):
        end = end + lengths_ref[doc]
        start = jnp.maximum(start, jnp.where(place >= end, end, 0))
    own_turns = jnp.broadcast_to(turns_ref[pl.ds(mine, 1), :], (rows, rows))
    turn = jnp.sum(jnp.where(row == column, own_turns, 0), axis=1, keepdims=True)
    for slot, shard in enumerate(slots_of(mine, count)):
        key_place = shard * rows + column
        allowed = (key_place <= place) & (key_place >= start)
        if slot:
            same_turn = turns_ref[pl.ds(shard, 1), :] == turn
            kept = jnp.full((rows, rows), blocks_ref[0, shard], jnp.int32) > 0
            allowed = allowed & (same_turn | kept)
        bias_ref[slot] = jnp.where(allowed, 0.0, masked_score)


def attend_kernel(groups, n_slots, columns, *refs):
    q_ref, bias_ref, weight_ref = refs[:3]
    pairs = refs[3 : 3 + n_slots]
    attended_ref, send_ref, keep_ref, scores_ref, rounded_ref = refs[3 + n_slots :]
    rows, dim = q_ref.shape[0], q_ref.shape[1] // groups
    factor = math.log2(math.e) / math.sqrt(dim)
    queries = jnp.concatenate([q_ref[:, g * dim : (g + 1) * dim] for g in range(groups)], axis=0)
    keys = jnp.concatenate([p[:rows] for p in pairs], axis=0)
    scores_ref[...] = lax.dot_general(
        queries, keys, (((1,), (1,)), ((), ())), preferred_element_type=jnp.float32
    )
    bias = jnp.concatenate([bias_ref[s] for s in range(n_slots)], axis=1)
    totals = []
    for g in range(groups):
        s = scores_ref[g * rows : (g + 1) * rows] + bias
        best = jnp.max(s, axis=1, keepdims=True)
        w = jnp.exp2((s - best) * factor)
        totals.append(jnp.sum(w, axis=1, keepdims=True))
        rounded_ref[g * rows : (g + 1) * rows] = w.astype(jnp.bfloat16)
    values = jnp.concatenate([p[rows:] for p in pairs], axis=0)
    summed = jnp.dot(rounded_ref[...], values, preferred_element_type=jnp.float32)
    for g in range(groups):
        attended_ref[:, g * dim : (g + 1) * dim] = (
            summed[g * rows : (g + 1) * rows] / totals[g]
        ).astype(jnp.bfloat16)
    project(attended_ref, weight_ref, send_ref, keep_ref, columns, 2)


def project(attended_ref, weight_ref, send_ref, keep_ref, columns, flip):
    mine = lax.axis_index("head") ^ flip
    attended = attended_ref[...]
    for ref, target in ((send_ref, mine ^ 1), (keep_ref, mine)):
        start = pl.multiple_of(target * columns, 128)
        ref[...] = jnp.dot(
            attended, weight_ref[:, pl.ds(start, columns)], preferred_element_type=jnp.float32
        ).astype(ref.dtype)


def project_kernel(columns, attended_ref, weight_ref, send_ref, keep_ref):
    project(attended_ref, weight_ref, send_ref, keep_ref, columns, 0)


def add_kernel(*refs):
    refs[-1][...] = sum(r[...].astype(jnp.float32) for r in refs[:-1]).astype(refs[-1].dtype)


def on_device(
    count, heads, queries, key_codes, value_codes, kv_scales, out_weight, turn_ids, block_mask, doc_lengths
):
    rows, dim = key_codes.shape
    groups = queries.shape[1] // dim
    columns = out_weight.shape[1] // heads
    bf16, f32 = jnp.bfloat16, jnp.float32
    small = pltpu.CompilerParams(vmem_limit_bytes=8 << 20)
    large = pltpu.CompilerParams(vmem_limit_bytes=24 << 20)

    pair = pl.pallas_call(
        dequantize_kernel,
        out_shape=jax.ShapeDtypeStruct((2 * rows, dim), bf16),
        in_specs=[whole(pltpu.SMEM), whole(), whole()],
        out_specs=whole(),
        compiler_params=small,
        cost_estimate=cost(4 * rows * dim, 8 * rows * dim),
    )(kv_scales.reshape(2), key_codes, value_codes)

    def moved(x, where):
        return lax.ppermute(x, "seq", [(i, where(i)) for i in range(count)])

    steps = range(1, count // 4 + 1)
    shifted = {step: moved(pair, lambda i: (i + 2 * step) % count) for step in reversed(steps)}
    pairs = [pair, moved(pair, lambda i: i ^ 1)]
    for step in steps:
        pairs += [shifted[step], moved(shifted[step], lambda i: i ^ 1)]
    n_slots = len(pairs)

    bias = pl.pallas_call(
        functools.partial(mask_kernel, count),
        out_shape=jax.ShapeDtypeStruct((n_slots, rows, rows), f32),
        in_specs=[whole(pltpu.SMEM), whole(pltpu.SMEM), whole()],
        out_specs=whole(),
        compiler_params=small,
        cost_estimate=cost(10 * n_slots * rows * rows, 4 * n_slots * rows * rows),
    )(doc_lengths, block_mask, turn_ids.reshape(count, rows))

    block = jax.ShapeDtypeStruct((rows, columns), bf16)
    wide = jax.ShapeDtypeStruct((rows, columns), f32)
    attended, send, keep = pl.pallas_call(
        functools.partial(attend_kernel, groups, n_slots, columns),
        out_shape=(jax.ShapeDtypeStruct((rows, groups * dim), bf16), block, wide),
        in_specs=[whole()] * (3 + n_slots),
        out_specs=(whole(),) * 3,
        scratch_shapes=[
            pltpu.VMEM((groups * rows, n_slots * rows), f32),
            pltpu.VMEM((groups * rows, n_slots * rows), bf16),
        ],
        compiler_params=large,
        cost_estimate=cost(4 * groups * rows * n_slots * rows * dim, 1 << 22),
    )(queries, bias, out_weight, *pairs)

    def swapped(x, bit):
        return lax.ppermute(x, "head", [(i, i ^ bit) for i in range(heads)])

    def total(*terms):
        return pl.pallas_call(
            add_kernel,
            out_shape=block,
            in_specs=[whole()] * len(terms),
            out_specs=whole(),
            compiler_params=small,
            cost_estimate=cost(rows * columns, 8 * rows * columns),
        )(*terms)

    far = swapped(total(keep, swapped(send, 1)), 2)
    near_send, near_keep = pl.pallas_call(
        functools.partial(project_kernel, columns),
        out_shape=(block, wide),
        in_specs=[whole()] * 2,
        out_specs=(whole(),) * 2,
        compiler_params=large,
        cost_estimate=cost(4 * rows * groups * dim * columns, 1 << 22),
    )(attended, out_weight)
    return total(near_keep, swapped(near_send, 1), far)


def solution(mesh):
    count, heads = mesh.shape["seq"], mesh.shape["head"]
    placed = (
        P("seq", "head"),
        P("seq", "head"),
        P("seq", "head"),
        P(None, "seq", "head"),
        P("head", None),
        P(),
        P("seq", None),
        P(),
    )
    return jax.shard_map(
        functools.partial(on_device, count, heads),
        mesh=mesh,
        in_specs=placed,
        out_specs=P("seq", "head"),
        check_vma=False,
    )
```
